512 devices in a mesh: row: 16 (over z_hi, y), col: 32 (over x, z_lo, core).
Axes of the slice: x: 4, y: 8, z: 8 (z_hi: 2, z_lo: 4; z = z_hi * 4 + z_lo), core: 2. Of those that a mesh axis runs over, the one named last changes fastest.
Arguments:
- spectra: bfloat16 [512, 3, 2, 2, 2048], P(('row', 'col')), may hold values from -6 to 6
- pair_source: int32 [8192], P(('row', 'col')), may hold values from 0 to 31
- pair_partner: int32 [8192], P(('row', 'col')), may hold values from 0 to 15
- pair_owner: int32 [8192], P(('row', 'col')), may hold values from 0 to 31, as said below
- pair_count: int32 [512], P(('row', 'col')), may hold values from 8 to 16, as said below
Outputs:
- stacked: bfloat16 [32768, 9, 1024], P(('row', 'col'))
The draws below stay inside these ranges and needn't reach their ends.
Inputs may be any that keep to these rules, and one draw needn't show every extreme that they name: `pair_owner`: among one device's 16 slots an owner is named 2 times or not at all, save at most one owner named fewer times; in each row of devices the first 2 slots of every device name one common owner. Slots j < pair_count of a device are active; some device has all 16 active and some has half.
All inputs are finite; a program needn't handle non-finite values.
Results may differ from the reference program's by a relative error of at most 0.0057.
Values may be sent and summed in bfloat16 or wider, within the bound.
A program may use at most 64 MiB of HBM per device.

```python
import math
import jax
import jax.numpy as jnp
from jax import lax

F = 2048
LAGS = 1024
SEG = 2
STA_DEV = 1
PAIR_DEV = 16
OWNERS = 32
BANDS = 16
STATIONS = 512
SOURCES = 32
PARTNERS = 16
CAP = 2
SLOTS = 8192
OUT_SLOTS = 32768


def draw_pair_count(key, part):
    key_counts, key_full, key_least = jax.random.split(jax.random.fold_in(key, 11), 3)
    device_total = BANDS * OWNERS
    counts = jax.random.randint(key_counts, (device_total,), PAIR_DEV // 2, PAIR_DEV + 1, dtype=jnp.int32)
    full_device = jax.random.randint(key_full, (), 0, device_total, dtype=jnp.int32)
    least_device = jax.random.randint(key_least, (), 0, device_total, dtype=jnp.int32)
    counts = counts.at[least_device].set(PAIR_DEV // 2)
    return counts.at[full_device].set(PAIR_DEV)


def owners_of_device(key_order, key_slots, star_owner):
    owner_order = jax.random.permutation(key_order, OWNERS).astype(jnp.int32)
    star_place = jnp.argmax(owner_order == star_owner)
    owner_order = owner_order.at[star_place].set(owner_order[0]).at[0].set(star_owner)
    shuffle = jax.random.permutation(key_slots, PAIR_DEV - CAP).astype(jnp.int32)
    other_owners = owner_order[1 + shuffle // CAP]
    lead_owners = jnp.full((CAP,), star_owner, jnp.int32)
    return jnp.concatenate([lead_owners, other_owners])


def draw_pair_owner(key, part):
    device_total = BANDS * OWNERS
    key_star, key_order, key_slots = jax.random.split(jax.random.fold_in(key, 23), 3)
    star_rows = jax.random.randint(key_star, (BANDS,), 0, OWNERS, dtype=jnp.int32)
    device_ids = jnp.arange(device_total, dtype=jnp.int32)
    star_each = star_rows[device_ids // OWNERS]
    order_keys = jax.random.split(key_order, device_total)
    slot_keys = jax.random.split(key_slots, device_total)
    owners = jax.vmap(owners_of_device)(order_keys, slot_keys, star_each)
    return owners.reshape(-1).astype(jnp.int32)


def set_ends(result, rng, smallest, largest):
    place = [jax.random.randint(jax.random.fold_in(rng, axis), (), 0, length) for axis, length in enumerate(result.shape)]
    widest = result.shape.index(max(result.shape))
    neighbour = place[:widest] + [(place[widest] + 1) % result.shape[widest]] + place[widest + 1:]
    return result.at[tuple(place)].set(smallest).at[tuple(neighbour)].set(largest)


def block_scale(rng, extent, shards, smallest, high):
    loudness = 1.0
    for position, parts in shards:
        steps = jax.random.uniform(jax.random.fold_in(jax.random.fold_in(rng, 6), position), (parts,), jnp.float32, smallest / len(shards), high / len(shards))
        loudness = loudness * jnp.repeat(jnp.exp(steps), extent[position] // parts).reshape((-1,) + (1,) * (len(extent) - 1 - position))
    return loudness


def centred(own_key, dims, scale, most, cuts=(), kind=jnp.bfloat16):
    result = scale * jax.random.normal(own_key, dims, jnp.float32)
    if cuts:
        result = result * block_scale(own_key, dims, cuts, -0.22, 0.18)
    return jnp.clip(result, -most, most).astype(kind)


def setup_inputs(seed: int = 0) -> dict:
    streams_of = jax.random.split(jax.random.key(seed), 6)
    return {
        "spectra": centred(streams_of[0], (STATIONS, 3, SEG, 2, F), 1.0, 6.0, ((0, 512),)),
        "pair_source": set_ends(jax.random.randint(streams_of[1], (SLOTS,), 0, SOURCES), jax.random.fold_in(streams_of[1], 1), 0, SOURCES - 1).astype(jnp.int32),
        "pair_partner": set_ends(jax.random.randint(streams_of[2], (SLOTS,), 0, PARTNERS), jax.random.fold_in(streams_of[2], 1), 0, PARTNERS - 1).astype(jnp.int32),
        "pair_owner": draw_pair_owner(jax.random.fold_in(streams_of[5], 71), 0),
        "pair_count": draw_pair_count(jax.random.fold_in(streams_of[5], 71), 0),
    }


def kernel_rows(freq_index, lag_count, freq_count, segments):
    offsets = jnp.arange(lag_count, dtype=jnp.int32) - lag_count // 2
    residue = jnp.mod(freq_index[:, None] * offsets[None, :], 2 * freq_count)
    angles = residue.astype(jnp.float32) * (math.pi / freq_count)
    weights = jnp.where(freq_index == 0, 1.0, 2.0).astype(jnp.float32) * (1.0 / math.sqrt(8.0 * segments * freq_count))
    cosine_table = (weights[:, None] * jnp.cos(angles)).astype(jnp.bfloat16)
    sine_table = (-weights[:, None] * jnp.sin(angles)).astype(jnp.bfloat16)
    return (cosine_table, sine_table)

def reference(spectra, pair_source, pair_partner, pair_owner, pair_count):
    cosine_table, sine_table = kernel_rows(jnp.arange(F, dtype=jnp.int32), LAGS, F, SEG)
    kernel_table = jnp.concatenate([cosine_table, sine_table], axis=0)
    slot_index = jnp.arange(PAIR_DEV, dtype=jnp.int32)

    def one_device(device):
        row_index = device // OWNERS
        col_index = device % OWNERS
        begin_at = (device * PAIR_DEV).astype(jnp.int32)
        source_local = lax.dynamic_slice_in_dim(pair_source, begin_at, PAIR_DEV)
        partner_local = lax.dynamic_slice_in_dim(pair_partner, begin_at, PAIR_DEV)
        owners = lax.dynamic_slice_in_dim(pair_owner, begin_at, PAIR_DEV)
        source_station = (row_index * OWNERS + source_local // STA_DEV) * STA_DEV + source_local % STA_DEV
        partner_station = (partner_local // STA_DEV * OWNERS + col_index) * STA_DEV + partner_local % STA_DEV
        source_spectra = spectra[source_station].astype(jnp.float32)
        partner_spectra = spectra[partner_station].astype(jnp.float32)
        rotated = jnp.stack([-partner_spectra[:, :, :, 1], partner_spectra[:, :, :, 0]], axis=3)
        real_part = jnp.einsum('pisqf,pjsqf->pijf', source_spectra, partner_spectra, precision=lax.Precision.HIGHEST)
        imag_part = jnp.einsum('pisqf,pjsqf->pijf', source_spectra, rotated, precision=lax.Precision.HIGHEST)
        active = (slot_index < pair_count[device]).astype(jnp.float32)
        spectral = jnp.stack([real_part, imag_part], axis=3) * active[:, None, None, None, None]
        spectral = spectral.reshape(PAIR_DEV * 9, 2 * F).astype(jnp.bfloat16)
        lagged = jnp.dot(spectral, kernel_table, preferred_element_type=jnp.float32).astype(jnp.bfloat16)
        matches = owners[:, None] == owners[None, :]
        earlier = slot_index[:, None] > slot_index[None, :]
        slot_rank = lax.optimization_barrier(jnp.sum(jnp.logical_and(matches, earlier).astype(jnp.int32), axis=1)).astype(jnp.int32)
        target_rows = ((row_index * OWNERS + owners) * OWNERS + col_index) * CAP + slot_rank
        return (lagged.reshape(PAIR_DEV, 9, LAGS), target_rows.astype(jnp.int32))
    all_lagged, all_rows = lax.map(one_device, jnp.arange(BANDS * OWNERS, dtype=jnp.int32))
    stacked = jnp.zeros((OUT_SLOTS, 9, LAGS), jnp.bfloat16)
    stacked = stacked.at[all_rows.reshape(-1)].set(all_lagged.reshape(-1, 9, LAGS))
    return stacked
```

```python
import math

import jax
import jax.numpy as jnp
import numpy as np
from jax import lax
from jax.experimental import pallas as pl
from jax.experimental.pallas import tpu as pltpu
from jax.sharding import PartitionSpec as P

MESH = pl.DeviceIdType.MESH
LAGS = 1024
FREQ = 2048
NX, NZL, NZH, NY = 4, 4, 2, 8
NZ = NZL * NZH
COLS = 32
ROWS = 16
SLOTS = 16
CHUNKS = 8
STEPS = FREQ // 16


def kernel(
    x_ref, base_ref, rot_ref, src_ref, par_ref, own_ref, cnt_ref,
    out_ref,
    abuf, bbuf, tab, state, xs, lhs, lag, sbuf,
    loc_sem, zs, zr, ys, yr, xsend, xrecv, ds, dr, es, er,
):
    row = lax.axis_index("row")
    col = lax.axis_index("col")
    zh = lax.div(row, NY)
    y = lax.rem(row, NY)
    x = lax.div(col, 8)
    zl = lax.rem(lax.div(col, 2), NZL)
    core = lax.rem(col, 2)
    z = zh * NZL + zl

    def dev(x_, y_, z_, c_):
        return (lax.div(z_, NZL) * NY + y_, x_ * 8 + lax.rem(z_, NZL) * 2 + c_)

    def zmod(v):
        return lax.rem(v + 2 * NZ, NZ)

    def ymod(v):
        return lax.rem(v + 2 * NY, NY)

    def xmod(v):
        return lax.rem(v + 2 * NX, NX)

    z_dev = {d: dev(x, y, zmod(z + d), core) for d in (1, -1)}
    y_dev = {d: dev(x, ymod(y + d), z, core) for d in (1, -1)}
    x_dev = {d: dev(xmod(x + d), y, z, core) for d in (1, -1)}
    c_dev = dev(x, y, z, 1 - core)

    def half(h):
        return pl.ds(6 * h, 6)

    def aslot(st, at):
        g = lax.rem(lax.div(st, NZL) + lax.div(at, NZL), 2)
        return (1 - g) * (x * 8 + lax.rem(st, NZL) * 2 + core) + g * (COLS + lax.rem(st, NZL))

    def remote(src, dst, s, r, target):
        return pltpu.make_async_remote_copy(
            src_ref=src, dst_ref=dst, send_sem=s, recv_sem=r, device_id=target, device_id_type=MESH
        )

    def halves(k, d):
        if k < 4:
            return (0, 1)
        return (0,) if d == 1 else (1,)

    DI = {1: 0, -1: 1}

    def z_copy(k, d, h):
        st = zmod(z - (k - 1) * d)
        nxt = zmod(z + d)
        src = x_ref.at[half(h)] if k == 1 else abuf.at[aslot(st, z), half(h)]
        if k < 4:
            dst = abuf.at[aslot(st, nxt), half(h)]
        else:
            dst = bbuf.at[lax.div(st, NZL) * NY + y, half(h)]
        return remote(src, dst, zs.at[DI[d], k - 1, h], zr.at[DI[d], k - 1, h], z_dev[d])

    def y_copy(m, k, d, h):
        st = ymod(y - (k - 1) * d)
        zhm = zh if m == 0 else 1 - zh
        idx = zhm * NY + st
        src = x_ref.at[half(h)] if (m == 0 and k == 1) else bbuf.at[idx, half(h)]
        return remote(
            src, bbuf.at[idx, half(h)], ys.at[m, DI[d], k - 1, h], yr.at[m, DI[d], k - 1, h], y_dev[d]
        )

    def x_copy(zi, k, d, h, own=False):
        xst = xmod(x - (k - 1) * d)
        idx = xst * 8 + zi * 2 + core
        src = x_ref.at[half(h)] if own else abuf.at[idx, half(h)]
        return remote(
            src, abuf.at[idx, half(h)], xsend.at[zi, DI[d], k - 1, h], xrecv.at[zi, DI[d], k - 1, h], x_dev[d]
        )

    def c_copy(xst, zi, own=False):
        idx = xst * 8 + zi * 2 + core
        src = x_ref if own else abuf.at[idx]
        q = xst * NZL + zi
        return remote(src, abuf.at[idx], ds.at[q], dr.at[q], c_dev)

    def z_start(k):
        for h in (0, 1):
            for d in (1, -1):
                if h in halves(k, d):
                    z_copy(k, d, h).start()

    def z_wait(k):
        for h in (0, 1):
            for d in (1, -1):
                if h in halves(k, d):
                    z_copy(k, d, h).wait_recv()

    def y_start(m, k):
        for h in (0, 1):
            for d in (1, -1):
                if h in halves(k, d):
                    y_copy(m, k, d, h).start()

    def y_wait(m, k):
        for h in (0, 1):
            for d in (1, -1):
                if h in halves(k, d):
                    y_copy(m, k, d, h).wait_recv()

    def near(k, body):
        if k == 0:
            body(zl)
        else:
            pl.when(zl >= k)(lambda: body(zl - k))
            pl.when(zl + k < NZL)(lambda: body(zl + k))

    def x_first(k):
        def body(zi):
            for h in (0, 1):
                for d in (1, -1):
                    x_copy(zi, 1, d, h, own=k == 0).start()
            c_copy(x, zi, own=k == 0).start()
        near(k, body)

    def x_second(k):
        def body(zi):
            for d, hh in ((1, 0), (-1, 1)):
                x_copy(zi, 1, d, hh).wait_recv()
                x_copy(zi, 2, d, hh).start()
            for d, hh in ((1, 1), (-1, 0)):
                x_copy(zi, 1, d, hh).wait_recv()
                c_copy(xmod(x - d), zi).start()
        near(k, body)

    def x_third(k):
        def body(zi):
            for d, hh in ((1, 0), (-1, 1)):
                x_copy(zi, 2, d, hh).wait_recv()
            c_copy(xmod(x + 2), zi).start()
        near(k, body)

    def table(chunk):
        per = STEPS // CHUNKS
        for part in range(4):
            lanes = pl.ds(part * 256, 256)
            rc = rot_ref[0, :, lanes]
            rs = rot_ref[1, :, lanes]

            def step(i, cs):
                c, s = cs
                f0 = pl.multiple_of((chunk * per + i) * 16, 16)
                tab[pl.ds(f0, 16), lanes] = c.astype(jnp.bfloat16)
                tab[pl.ds(FREQ + f0, 16), lanes] = s.astype(jnp.bfloat16)
                return (c * rc + s * rs, s * rc - c * rs)

            if chunk == 0:
                init = (base_ref[0, :, lanes], base_ref[1, :, lanes])
            else:
                init = (state[0, :, lanes], state[1, :, lanes])
            c, s = lax.fori_loop(0, per, step, init)
            state[0, :, lanes] = c
            state[1, :, lanes] = s
        if chunk == 0:
            rows = lax.broadcasted_iota(jnp.int32, (16, LAGS), 0)
            weight = jnp.where(rows == 0, 0.5, 1.0)
            tab[pl.ds(0, 16), :] = (base_ref[0] * weight).astype(jnp.bfloat16)
            tab[pl.ds(FREQ, 16), :] = (base_ref[1] * weight).astype(jnp.bfloat16)

    barrier = pltpu.get_barrier_semaphore()
    targets = [z_dev[1], z_dev[-1], y_dev[1], y_dev[-1], x_dev[1], x_dev[-1], c_dev]
    for t in targets:
        pl.semaphore_signal(barrier, inc=1, device_id=t, device_id_type=MESH)
    own_a = pltpu.make_async_copy(x_ref, abuf.at[col], loc_sem.at[0])
    own_b = pltpu.make_async_copy(x_ref, bbuf.at[row], loc_sem.at[1])
    own_a.start()
    own_b.start()
    pl.semaphore_wait(barrier, len(targets))

    z_start(1)
    y_start(0, 1)
    x_first(0)
    table(0)
    for k in (1, 2, 3):
        z_wait(k)
        z_start(k + 1)
        y_wait(0, k)
        y_start(0, k + 1)
        x_first(k)
        x_second(k - 1)
        if k >= 2:
            x_third(k - 2)
        table(k)
    z_wait(4)
    y_start(1, 1)
    y_wait(0, 4)
    x_second(3)
    x_third(2)
    table(4)
    y_wait(1, 1)
    y_start(1, 2)
    x_third(3)
    table(5)
    y_wait(1, 2)
    y_start(1, 3)
    table(6)
    y_wait(1, 3)
    y_start(1, 4)
    table(7)

    owners = [own_ref[j] for j in range(SLOTS)]
    rows64 = lax.broadcasted_iota(jnp.int32, (64, SLOTS), 0)
    cols16 = lax.broadcasted_iota(jnp.int32, (64, SLOTS), 1)
    goal = jnp.zeros((64, SLOTS), jnp.int32)
    for j in range(SLOTS):
        rank = jnp.int32(0)
        for j2 in range(j):
            rank = rank + (owners[j] == owners[j2]).astype(jnp.int32)
        goal = jnp.where(cols16 == j, owners[j] * 2 + rank, goal)
    onehot = (goal == rows64).astype(jnp.float32).astype(jnp.bfloat16)

    y_wait(1, 4)
    for q in range(NX * NZL):
        xst, zi = q // NZL, q % NZL
        c_copy(xst, zi).wait_recv()
    own_a.wait()
    own_b.wait()

    count = cnt_ref[0]

    def cross(p, _):
        a = abuf[src_ref[p]].astype(jnp.float32)
        b = bbuf[par_ref[p]].astype(jnp.float32)
        act = jnp.where(p < count, jnp.float32(1.0), jnp.float32(0.0))
        for i in range(3):
            for j in range(3):
                re = None
                im = None
                for s in range(2):
                    ar, ai = a[i * 4 + s * 2], a[i * 4 + s * 2 + 1]
                    br, bi = b[j * 4 + s * 2], b[j * 4 + s * 2 + 1]
                    rt = ar * br + ai * bi
                    it = ai * br - ar * bi
                    re = rt if re is None else re + rt
                    im = it if im is None else im + it
                at = pl.multiple_of(((i * 3 + j) * SLOTS + p) * 32, 32)
                xs[pl.ds(at, 16), :] = re * act
                xs[pl.ds(at + 16, 16), :] = im * act
        return 0

    lax.fori_loop(0, SLOTS, cross, 0)

    def pack(g, _):
        for kk in range(32):
            v = xs[pl.ds(g * 512 + kk, 16, stride=32), :]
            lhs[pl.ds(pl.multiple_of(g * 16, 16), 16), pl.ds(kk * 128, 128)] = v.astype(jnp.bfloat16)
        return 0

    lax.fori_loop(0, 9, pack, 0)

    def mm(n, _):
        lanes = pl.ds(pl.multiple_of(n * 256, 256), 256)
        acc = jnp.dot(lhs[...], tab[:, lanes], preferred_element_type=jnp.float32)
        lag[:, lanes] = acc.astype(jnp.bfloat16)
        return 0

    lax.fori_loop(0, 4, mm, 0)

    def place(k, _):
        part = lag[pl.ds(pl.multiple_of(k * SLOTS, SLOTS), SLOTS), :]
        v = jnp.dot(onehot, part, preferred_element_type=jnp.float32).astype(jnp.bfloat16)
        sbuf[:, k] = v.reshape(COLS, 2, LAGS)
        return 0

    lax.fori_loop(0, 9, place, 0)

    def e_copy(i):
        to = lax.rem(col + i, COLS)
        return remote(sbuf.at[to], out_ref.at[col], es.at[i - 1], er.at[i - 1], (row, to))

    for i in range(1, COLS):
        e_copy(i).start()
    mine = pltpu.make_async_copy(sbuf.at[col], out_ref.at[col], loc_sem.at[2])
    mine.start()

    for k in (1, 2, 3, 4):
        for d in (1, -1):
            for h in halves(k, d):
                z_copy(k, d, h).wait_send()
                for m in (0, 1):
                    y_copy(m, k, d, h).wait_send()
    for zi in range(NZL):
        for h in (0, 1):
            for d in (1, -1):
                x_copy(zi, 1, d, h).wait_send()
        x_copy(zi, 2, 1, 0).wait_send()
        x_copy(zi, 2, -1, 1).wait_send()
    for q in range(NX * NZL):
        c_copy(q // NZL, q % NZL).wait_send()
    for i in range(1, COLS):
        e_copy(i).wait_recv()
    for i in range(1, COLS):
        e_copy(i).wait_send()
    mine.wait()


def twiddles():
    scale = 2.0 / math.sqrt(16.0 * FREQ)
    u = np.arange(LAGS) - LAGS // 2
    f = np.arange(16)
    m = np.mod(f[:, None] * u[None, :], 2 * FREQ) * (math.pi / FREQ)
    base = np.stack([np.cos(m), -np.sin(m)]) * scale
    r = np.mod(16 * u, 2 * FREQ) * (math.pi / FREQ)
    rot = np.stack([np.cos(r), np.sin(r)])[:, None, :] * np.ones((1, 16, 1))
    return base.astype(np.float32), rot.astype(np.float32)


def body(spectra, pair_source, pair_partner, pair_owner, pair_count):
    base, rot = twiddles()
    station = spectra.reshape(12, 16, 128)
    vmem = pl.BlockSpec(memory_space=pltpu.VMEM)
    smem = pl.BlockSpec(memory_space=pltpu.SMEM)
    dma = pltpu.SemaphoreType.DMA
    out = pl.pallas_call(
        kernel,
        out_shape=jax.ShapeDtypeStruct((COLS, 9, 2, LAGS), jnp.bfloat16),
        in_specs=[vmem, vmem, vmem, smem, smem, smem, smem],
        out_specs=pl.BlockSpec(memory_space=pl.ANY),
        scratch_shapes=[
            pltpu.VMEM((COLS + NZL, 12, 16, 128), jnp.bfloat16),
            pltpu.VMEM((ROWS, 12, 16, 128), jnp.bfloat16),
            pltpu.VMEM((2 * FREQ, LAGS), jnp.bfloat16),
            pltpu.VMEM((2, 16, LAGS), jnp.float32),
            pltpu.VMEM((144 * 32, 128), jnp.float32),
            pltpu.VMEM((144, 2 * FREQ), jnp.bfloat16),
            pltpu.VMEM((144, LAGS), jnp.bfloat16),
            pltpu.VMEM((COLS, 9, 2, LAGS), jnp.bfloat16),
            dma((3,)),
            dma((2, 4, 2)), dma((2, 4, 2)),
            dma((2, 2, 4, 2)), dma((2, 2, 4, 2)),
            dma((4, 2, 2, 2)), dma((4, 2, 2, 2)),
            dma((16,)), dma((16,)),
            dma((31,)), dma((31,)),
        ],
        compiler_params=pltpu.CompilerParams(
            collective_id=0, has_side_effects=True, vmem_limit_bytes=48 * 1024 * 1024
        ),
    )(station, jnp.asarray(base), jnp.asarray(rot), pair_source, pair_partner, pair_owner, pair_count)
    return out.transpose(0, 2, 1, 3).reshape(COLS * 2, 9, LAGS)


def solution(mesh):
    placed = (
        P(("row", "col"), None, None, None, None),
        P(("row", "col")),
        P(("row", "col")),
        P(("row", "col")),
        P(("row", "col")),
    )
    return jax.shard_map(
        body, mesh=mesh, in_specs=placed, out_specs=P(("row", "col"), None, None), check_vma=False
    )
```

```python
import math

import jax
import jax.numpy as jnp
import numpy as np
from jax import lax
from jax.experimental import pallas as pl
from jax.experimental.pallas import tpu as pltpu
from jax.sharding import PartitionSpec as P

MESH = pl.DeviceIdType.MESH
LAGS = 1024
FREQ = 2048
NX, NZL, NZH, NY = 4, 4, 2, 8
COLS = 32
ROWS = 16
SLOTS = 16
CHUNKS = 8
STEPS = FREQ // 16
PITCH = 40


def kernel(
    x_ref, int_ref,
    out_ref,
    abuf, bown, bpar, tab, state, xs, lhs, lag, sbuf, base_ref, rot_ref, pint, sint,
    loc_sem, zs, zr, ys, yr, vs, vr, xsend, xrecv, ds, dr, es, er,
):
    row = lax.axis_index("row")
    col = lax.axis_index("col")
    zh = lax.div(row, NY)
    y = lax.rem(row, NY)
    x = lax.div(col, 8)
    zl = lax.rem(lax.div(col, 2), NZL)
    core = lax.rem(col, 2)

    def dev(x_, y_, zh_, zl_, c_):
        return (zh_ * NY + y_, x_ * 8 + zl_ * 2 + c_)

    def ymod(v):
        return lax.rem(v + 2 * NY, NY)

    def xmod(v):
        return lax.rem(v + 2 * NX, NX)

    y_dev = {d: dev(x, ymod(y + d), zh, zl, core) for d in (1, -1, 2, -2)}
    x_dev = {d: dev(xmod(x + d), y, zh, zl, core) for d in (1, -1, 2)}
    c_dev = dev(x, y, zh, zl, 1 - core)
    zp = lax.rem(zl + 2, NZL)
    p_dev = dev(x, y, zh, zp, core)
    pcol = x * 8 + zp * 2 + core
    o_dev = dev(x, y, 1 - zh, zl, core)
    f_dev = dev(x, y, 1 - zh, zp, core)

    def half(h):
        return pl.ds(6 * h, 6)

    def remote(src, dst, s, r, target):
        return pltpu.make_async_remote_copy(
            src_ref=src, dst_ref=dst, send_sem=s, recv_sem=r, device_id=target, device_id_type=MESH
        )

    def halves(k, d):
        if k < 4:
            return (0, 1)
        return (0,) if d == 1 else (1,)

    DI = {1: 0, -1: 1}
    XI = {1: 0, -1: 1, 2: 2}

    def near(k, body):
        if k == 0:
            body(zl)
        else:
            pl.when(zl >= k)(lambda: body(zl - k))
            pl.when(zl + k < NZL)(lambda: body(zl + k))

    def z_send(zi):
        return remote(x_ref, abuf.at[col], zs.at[zi], zr.at[zl], dev(x, y, zh, zi, core))

    def z_recv(zi):
        return remote(x_ref, abuf.at[x * 8 + zi * 2 + core], zs.at[zi], zr.at[zi], dev(x, y, zh, zi, core))

    def o_copy():
        return remote(x_ref, bown.at[row], zs.at[NZL], zr.at[NZL], o_dev)

    def f_copy():
        return remote(x_ref, bpar.at[row], zs.at[NZL + 1], zr.at[NZL + 1], f_dev)

    def i_copy():
        return remote(int_ref, pint, zs.at[NZL + 2], zr.at[NZL + 2], p_dev)

    def y_copy(m, k, d, h):
        buf = bown if m == 0 else bpar
        idx = (1 - zh if m == 2 else zh) * NY + ymod(y - (k - 1) * d)
        if k == 1 and m < 2:
            src = x_ref.at[half(h)] if m == 0 else abuf.at[pcol, half(h)]
        else:
            src = buf.at[idx, half(h)]
        return remote(
            src, buf.at[idx, half(h)], ys.at[m, DI[d], k - 1, h], yr.at[m, DI[d], k - 1, h], y_dev[d]
        )

    def v_copy(j, d):
        idx = (1 - zh) * NY + (y if j < 3 else ymod(y - 2 * d))
        ref = bown.at[idx, half(0 if d == 1 else 1)] if j == 4 else bown.at[idx]
        return remote(ref, ref, vs.at[DI[d], j - 1], vr.at[DI[d], j - 1], y_dev[d if j in (1, 3) else 2 * d])

    def v_first():
        for j in (2, 1):
            for d in (1, -1):
                v_copy(j, d).start()

    def v_second():
        for d in (1, -1):
            v_copy(2, d).wait_recv()
            v_copy(3, d).start()
            v_copy(4, d).start()

    def v_last():
        for d in (1, -1):
            for j in (1, 3, 4):
                v_copy(j, d).wait_recv()

    def x_copy(zi, d, own=False):
        idx = x * 8 + zi * 2 + core
        src = x_ref if own else abuf.at[idx]
        return remote(src, abuf.at[idx], xsend.at[zi, XI[d]], xrecv.at[zi, XI[d]], x_dev[d])

    def c_copy(xst, zi, own=False):
        idx = xst * 8 + zi * 2 + core
        src = x_ref if own else abuf.at[idx]
        q = xst * NZL + zi
        return remote(src, abuf.at[idx], ds.at[q], dr.at[q], c_dev)

    def y_start(m, k):
        for h in (0, 1):
            for d in (1, -1):
                if h in halves(k, d):
                    y_copy(m, k, d, h).start()

    def y_next(m, k):
        for h in (0, 1):
            for d in (1, -1):
                if h in halves(k, d):
                    y_copy(m, k, d, h).wait_recv()
                    if k < 4 and h in halves(k + 1, d):
                        y_copy(m, k + 1, d, h).start()

    def x_first(k):
        def body(zi):
            if k:
                z_recv(zi).wait_recv()
            for d in (2, 1, -1):
                x_copy(zi, d, own=k == 0).start()
            c_copy(x, zi, own=k == 0).start()
        near(k, body)

    def x_second(k):
        def body(zi):
            for d in (1, -1, 2):
                x_copy(zi, d).wait_recv()
                c_copy(xmod(x - d), zi).start()
        near(k, body)

    def table(chunk):
        per = STEPS // CHUNKS
        for part in range(4):
            lanes = pl.ds(part * 256, 256)
            rc = jnp.concatenate([rot_ref[0, :, lanes]] * 2, axis=0)
            rs = jnp.concatenate([rot_ref[1, :, lanes]] * 2, axis=0)

            def step(i, cs):
                c, s = cs
                f0 = pl.multiple_of((chunk * per + i) * 16, 16)
                tab[pl.ds(f0, 16), lanes] = c.astype(jnp.bfloat16)
                tab[pl.ds(FREQ + f0, 16), lanes] = s.astype(jnp.bfloat16)
                return (c * rc + s * rs, s * rc - c * rs)

            if chunk == 0:
                init = (base_ref[0, :, lanes], base_ref[1, :, lanes])
            else:
                init = (state[0, :, lanes], state[1, :, lanes])
            c, s = lax.fori_loop(0, per, step, init)
            state[0, :, lanes] = c
            state[1, :, lanes] = s
        if chunk == 0:
            rows = lax.broadcasted_iota(jnp.int32, (16, LAGS), 0)
            weight = jnp.where(rows == 0, 0.5, 1.0)
            tab[pl.ds(0, 16), :] = (base_ref[0] * weight).astype(jnp.bfloat16)
            tab[pl.ds(FREQ, 16), :] = (base_ref[1] * weight).astype(jnp.bfloat16)

    own = [
        pltpu.make_async_copy(x_ref, abuf.at[col], loc_sem.at[0]),
        pltpu.make_async_copy(x_ref, bown.at[row], loc_sem.at[1]),
    ]
    barrier = pltpu.get_barrier_semaphore()
    targets = list(y_dev.values()) + list(x_dev.values()) + [c_dev, o_dev, f_dev]
    targets += [dev(x, y, zh, lax.rem(zl + j, NZL), core) for j in range(1, NZL)]
    for t in targets:
        pl.semaphore_signal(barrier, inc=1, device_id=t, device_id_type=MESH)
    for c in own:
        c.start()
    for part in range(4):
        lanes = pl.ds(part * 256, 256)
        for dst, n in ((base_ref, 16), (rot_ref, 8)):
            shape = (n, 256)
            f = lax.broadcasted_iota(jnp.int32, shape, 0) if n == 16 else jnp.full(shape, 16, jnp.int32)
            lag_of = lax.broadcasted_iota(jnp.int32, shape, 1) + (part * 256 - LAGS // 2)
            angle = jnp.bitwise_and(f * lag_of, 2 * FREQ - 1).astype(jnp.float32) * (math.pi / FREQ)
            size = 2.0 / math.sqrt(16.0 * FREQ) if n == 16 else 1.0
            dst[0, :, lanes] = jnp.cos(angle) * size
            dst[1, :, lanes] = jnp.sin(angle) * (-size if n == 16 else size)
    pl.semaphore_wait(barrier, len(targets))

    ints = [
        pltpu.make_async_copy(int_ref, sint.at[0], loc_sem.at[2]),
        pltpu.make_async_copy(pint, sint.at[1], loc_sem.at[3]),
    ]
    beside = pltpu.make_async_copy(abuf.at[pcol], bpar.at[row], loc_sem.at[4])

    i_copy().start()
    ints[0].start()
    near(1, lambda zi: z_send(zi).start())
    o_copy().start()
    near(2, lambda zi: z_send(zi).start())
    f_copy().start()
    near(3, lambda zi: z_send(zi).start())
    y_start(0, 1)
    x_first(0)
    table(0)
    x_first(1)
    o_copy().wait_recv()
    v_first()
    y_next(0, 1)
    x_first(2)
    y_start(1, 1)
    beside.start()
    table(1)
    f_copy().wait_recv()
    y_start(2, 1)
    i_copy().wait_recv()
    ints[1].start()
    x_first(3)
    y_next(0, 2)
    x_second(0)
    table(2)
    v_second()
    y_next(1, 1)
    x_second(1)
    y_next(2, 1)
    table(3)
    y_next(0, 3)
    x_second(2)
    table(4)
    y_next(1, 2)
    y_next(2, 2)
    table(5)
    x_second(3)
    table(6)
    table(7)
    for c in ints:
        c.wait()

    rows = lax.broadcasted_iota(jnp.int32, (2 * 16, SLOTS), 0)
    cols = lax.broadcasted_iota(jnp.int32, (2 * 16, SLOTS), 1)
    onehots = []
    for sel in range(2):
        goal = jnp.full((2 * 16, SLOTS), -1, jnp.int32)
        owners = [sint[sel, 0, j] for j in range(SLOTS)]
        for j in range(SLOTS):
            o = owners[j]
            rank = jnp.int32(0)
            for j2 in range(j):
                rank = rank + (o == owners[j2]).astype(jnp.int32)
            ozl = lax.rem(lax.div(o, 2), NZL)
            place = lax.div(o, 8) * 4 + lax.rem(ozl, 2) * 2 + lax.rem(o, 2)
            here = lax.div(ozl, 2) == lax.div(zl, 2)
            at = jnp.where(here, place * 2 + rank, jnp.int32(-1))
            goal = jnp.where(cols == j, at, goal)
        onehots.append((goal == rows).astype(jnp.float32).astype(jnp.bfloat16))

    me = x * 4 + lax.rem(zl, 2) * 2 + core
    columns = (col, pcol)

    def e_copy(i, sel):
        to = lax.rem(me + i, 16)
        tcol = lax.div(to, 4) * 8 + (lax.div(zl, 2) * 2 + lax.rem(lax.div(to, 2), 2)) * 2 + lax.rem(to, 2)
        return remote(
            sbuf.at[sel, to], out_ref.at[:, columns[sel]], es.at[i - 1, sel], er.at[i - 1, sel], (row, tcol)
        )

    def compute(sel, between):
        def cross(p, _):
            a = abuf[sint[sel, 0, SLOTS + p]].astype(jnp.float32)
            b = (bown, bpar)[sel][sint[sel, 0, 2 * SLOTS + p]].astype(jnp.float32)
            act = jnp.where(p < sint[sel, 0, 3 * SLOTS], jnp.float32(1.0), jnp.float32(0.0))
            for i in range(3):
                for j in range(3):
                    re = None
                    im = None
                    for s in range(2):
                        ar, ai = a[i * 4 + s * 2], a[i * 4 + s * 2 + 1]
                        br, bi = b[j * 4 + s * 2], b[j * 4 + s * 2 + 1]
                        rt = ar * br + ai * bi
                        it = ai * br - ar * bi
                        re = rt if re is None else re + rt
                        im = it if im is None else im + it
                    at = pl.multiple_of(((i * 3 + j) * SLOTS + p) * PITCH, 8)
                    xs[pl.ds(at, 16), :] = re * act
                    xs[pl.ds(at + 16, 16), :] = im * act
            return 0

        def pack(g, _):
            for kk in range(32):
                v = xs[pl.ds(g * (16 * PITCH) + kk, 16, stride=PITCH), :]
                lhs[pl.ds(pl.multiple_of(g * 16, 16), 16), pl.ds(kk * 128, 128)] = v.astype(jnp.bfloat16)
            return 0

        def mm(n, _):
            lanes = pl.ds(pl.multiple_of(n * 256, 256), 256)
            acc = jnp.dot(lhs[...], tab[:, lanes], preferred_element_type=jnp.float32)
            lag[:, lanes] = acc.astype(jnp.bfloat16)
            return 0

        lax.fori_loop(0, SLOTS, cross, 0)
        lax.fori_loop(0, 9, pack, 0)
        lax.fori_loop(0, 2, mm, 0)
        between()
        lax.fori_loop(2, 4, mm, 0)
        for k in range(9):
            part = lag[pl.ds(k * SLOTS, SLOTS), :]
            v = jnp.dot(onehots[sel], part, preferred_element_type=jnp.float32).astype(jnp.bfloat16)
            sbuf[sel, :, k] = v.reshape(16, 2, LAGS)
        for i in range(1, 16):
            e_copy(i, sel).start()
        mine[sel].start()

    mine = [
        pltpu.make_async_copy(sbuf.at[sel, me], out_ref.at[:, columns[sel]], loc_sem.at[5 + sel])
        for sel in range(2)
    ]
    v_last()
    y_next(0, 4)
    for q in range(NX * NZL):
        c_copy(q // NZL, q % NZL).wait_recv()
    for c in own:
        c.wait()

    def relay():
        y_next(1, 3)
        y_next(2, 3)

    compute(0, relay)
    y_next(1, 4)
    y_next(2, 4)
    beside.wait()
    compute(1, lambda: None)

    o_copy().wait_send()
    f_copy().wait_send()
    i_copy().wait_send()
    for k in (1, 2, 3):
        near(k, lambda zi: z_send(zi).wait_send())
    for k in (1, 2, 3, 4):
        for d in (1, -1):
            for h in halves(k, d):
                for m in range(3):
                    y_copy(m, k, d, h).wait_send()
            v_copy(k, d).wait_send()
    for zi in range(NZL):
        for d in (1, -1, 2):
            x_copy(zi, d).wait_send()
    for q in range(NX * NZL):
        c_copy(q // NZL, q % NZL).wait_send()
    for i in range(1, 16):
        for sel in range(2):
            e_copy(i, sel).wait_recv()
    for i in range(1, 16):
        for sel in range(2):
            e_copy(i, sel).wait_send()
    for c in mine:
        c.wait()


def body(spectra, pair_source, pair_partner, pair_owner, pair_count):
    station = spectra.reshape(12, 16, 128)
    ints = jnp.concatenate(
        [pair_owner, pair_source, pair_partner, pair_count, jnp.zeros(127 - 3 * SLOTS, jnp.int32)]
    )
    vmem = pl.BlockSpec(memory_space=pltpu.VMEM)
    dma = pltpu.SemaphoreType.DMA
    out = pl.pallas_call(
        kernel,
        out_shape=jax.ShapeDtypeStruct((9, COLS, 2, LAGS), jnp.bfloat16),
        in_specs=[vmem, vmem],
        out_specs=pl.BlockSpec(memory_space=pl.ANY),
        scratch_shapes=[
            pltpu.VMEM((COLS, 12, 16, 128), jnp.bfloat16),
            pltpu.VMEM((ROWS, 12, 16, 128), jnp.bfloat16),
            pltpu.VMEM((ROWS, 12, 16, 128), jnp.bfloat16),
            pltpu.VMEM((2 * FREQ, LAGS), jnp.bfloat16),
            pltpu.VMEM((2, 16, LAGS), jnp.float32),
            pltpu.VMEM((9 * SLOTS * PITCH, 128), jnp.float32),
            pltpu.VMEM((9 * SLOTS, 2 * FREQ), jnp.bfloat16),
            pltpu.VMEM((9 * SLOTS, LAGS), jnp.bfloat16),
            pltpu.VMEM((2, 16, 9, 2, LAGS), jnp.bfloat16),
            pltpu.VMEM((2, 16, LAGS), jnp.float32),
            pltpu.VMEM((2, 8, LAGS), jnp.float32),
            pltpu.VMEM((1, 128), jnp.int32),
            pltpu.SMEM((2, 1, 128), jnp.int32),
            dma((7,)),
            dma((NZL + 3,)), dma((NZL + 3,)),
            dma((3, 2, 4, 2)), dma((3, 2, 4, 2)),
            dma((2, 4)), dma((2, 4)),
            dma((NZL, 3)), dma((NZL, 3)),
            dma((16,)), dma((16,)),
            dma((15, 2)), dma((15, 2)),
        ],
        compiler_params=pltpu.CompilerParams(
            collective_id=0, has_side_effects=True, vmem_limit_bytes=48 * 1024 * 1024
        ),
    )(station, ints.reshape(1, 128))
    return out.reshape(9, COLS * 2, LAGS).transpose(1, 0, 2)


def solution(mesh):
    placed = (
        P(("row", "col"), None, None, None, None),
        P(("row", "col")),
        P(("row", "col")),
        P(("row", "col")),
        P(("row", "col")),
    )
    return jax.shard_map(
        body, mesh=mesh, in_specs=placed, out_specs=P(("row", "col"), None, None), check_vma=False
    )
```

```python
import math

import jax
import jax.numpy as jnp
import numpy as np
from jax import lax
from jax.experimental import pallas as pl
from jax.experimental.pallas import tpu as pltpu
from jax.sharding import PartitionSpec as P

MESH = pl.DeviceIdType.MESH
LAGS = 1024
FREQ = 2048
NX, NZL, NZH, NY = 4, 4, 2, 8
COLS = 32
ROWS = 16
SLOTS = 16
CHUNKS = 8
STEPS = FREQ // 16
PITCH = 40


def kernel(
    x_ref, int_ref,
    out_ref,
    abuf, bown, bpar, tab, state, xs, lhs, lag, sbuf, base_ref, rot_ref, pint, sint,
    loc_sem, zs, zr, ts, tr, hs, hr, xsend, xrecv, ds, dr, es, er,
):
    row = lax.axis_index("row")
    col = lax.axis_index("col")
    zh = lax.div(row, NY)
    y = lax.rem(row, NY)
    x = lax.div(col, 8)
    zl = lax.rem(lax.div(col, 2), NZL)
    core = lax.rem(col, 2)

    def dev(x_, y_, zh_, zl_, c_):
        return (zh_ * NY + y_, x_ * 8 + zl_ * 2 + c_)

    def ymod(v):
        return lax.rem(v + 2 * NY, NY)

    def xmod(v):
        return lax.rem(v + 2 * NX, NX)

    y_dev = {d: dev(x, ymod(y + d), zh, zl, core) for d in (1, -1, 2, -2)}
    x_dev = {d: dev(xmod(x + d), y, zh, zl, core) for d in (1, -1, 2)}
    c_dev = dev(x, y, zh, zl, 1 - core)
    zp = lax.rem(zl + 2, NZL)
    p_dev = dev(x, y, zh, zp, core)
    pcol = x * 8 + zp * 2 + core
    o_dev = dev(x, y, 1 - zh, zl, core)
    f_dev = dev(x, y, 1 - zh, zp, core)

    def half(h):
        return pl.ds(6 * h, 6)

    def remote(src, dst, s, r, target):
        return pltpu.make_async_remote_copy(
            src_ref=src, dst_ref=dst, send_sem=s, recv_sem=r, device_id=target, device_id_type=MESH
        )

    DI = {1: 0, -1: 1}
    XI = {1: 0, -1: 1, 2: 2}

    def kinds(m):
        return (1, 2) if m == 2 else (1, 2, 3, 4)

    def near(k, body):
        if k == 0:
            body(zl)
        else:
            pl.when(zl >= k)(lambda: body(zl - k))
            pl.when(zl + k < NZL)(lambda: body(zl + k))

    def z_send(zi):
        return remote(x_ref, abuf.at[col], zs.at[zi], zr.at[zl], dev(x, y, zh, zi, core))

    def z_recv(zi):
        return remote(x_ref, abuf.at[x * 8 + zi * 2 + core], zs.at[zi], zr.at[zi], dev(x, y, zh, zi, core))

    def o_copy():
        return remote(x_ref, bown.at[row], zs.at[NZL], zr.at[NZL], o_dev)

    def f_copy():
        return remote(x_ref, bpar.at[row], zs.at[NZL + 1], zr.at[NZL + 1], f_dev)

    def i_copy():
        return remote(int_ref, pint, zs.at[NZL + 2], zr.at[NZL + 2], p_dev)

    def t_copy(m, j, d):
        buf = bown if m < 2 else bpar
        back = (0, 0 if m < 2 else 1, 2, 2)[j - 1]
        idx = (zh if m % 2 == 0 else 1 - zh) * NY + ymod(y - back * d)
        dst = buf.at[idx, half(0 if d == 1 else 1)] if j == 4 else buf.at[idx]
        src = dst
        if back == 0 and m == 0:
            src = x_ref
        elif back == 0 and m == 2:
            src = abuf.at[pcol]
        far = 2 if j == 4 or (j == 2 and m < 2) else 1
        return remote(src, dst, ts.at[m, DI[d], j - 1], tr.at[m, DI[d], j - 1], y_dev[far * d])

    def t_start(m, *js):
        for j in js:
            for d in (1, -1):
                t_copy(m, j, d).start()

    def t_wait(m, *js):
        for j in js:
            for d in (1, -1):
                t_copy(m, j, d).wait_recv()

    def t_pass(m, j, *js):
        for d in (1, -1):
            t_copy(m, j, d).wait_recv()
            for j2 in js:
                t_copy(m, j2, d).start()

    def h_copy(q):
        idx = zh * NY + ymod(y + (3, -3, 4)[q])
        return remote(bown.at[idx], bpar.at[idx], hs.at[q], hr.at[q], p_dev)

    def x_copy(zi, d, own=False):
        idx = x * 8 + zi * 2 + core
        src = x_ref if own else abuf.at[idx]
        return remote(src, abuf.at[idx], xsend.at[zi, XI[d]], xrecv.at[zi, XI[d]], x_dev[d])

    def c_copy(xst, zi, own=False):
        idx = xst * 8 + zi * 2 + core
        src = x_ref if own else abuf.at[idx]
        q = xst * NZL + zi
        return remote(src, abuf.at[idx], ds.at[q], dr.at[q], c_dev)

    def x_first(k):
        def body(zi):
            if k:
                z_recv(zi).wait_recv()
            for d in (2, 1, -1):
                x_copy(zi, d, own=k == 0).start()
            c_copy(x, zi, own=k == 0).start()
        near(k, body)

    def x_second(k):
        def body(zi):
            for d in (1, -1, 2):
                x_copy(zi, d).wait_recv()
                c_copy(xmod(x - d), zi).start()
        near(k, body)

    def table(chunk):
        per = STEPS // CHUNKS
        for part in range(4):
            lanes = pl.ds(part * 256, 256)
            rc = jnp.concatenate([rot_ref[0, :, lanes]] * 2, axis=0)
            rs = jnp.concatenate([rot_ref[1, :, lanes]] * 2, axis=0)

            def step(i, cs):
                c, s = cs
                f0 = pl.multiple_of((chunk * per + i) * 16, 16)
                tab[pl.ds(f0, 16), lanes] = c.astype(jnp.bfloat16)
                tab[pl.ds(FREQ + f0, 16), lanes] = s.astype(jnp.bfloat16)
                return (c * rc + s * rs, s * rc - c * rs)

            if chunk == 0:
                init = (base_ref[0, :, lanes], base_ref[1, :, lanes])
            else:
                init = (state[0, :, lanes], state[1, :, lanes])
            c, s = lax.fori_loop(0, per, step, init)
            state[0, :, lanes] = c
            state[1, :, lanes] = s
        if chunk == 0:
            rows = lax.broadcasted_iota(jnp.int32, (16, LAGS), 0)
            weight = jnp.where(rows == 0, 0.5, 1.0)
            tab[pl.ds(0, 16), :] = (base_ref[0] * weight).astype(jnp.bfloat16)
            tab[pl.ds(FREQ, 16), :] = (base_ref[1] * weight).astype(jnp.bfloat16)

    own = [
        pltpu.make_async_copy(x_ref, abuf.at[col], loc_sem.at[0]),
        pltpu.make_async_copy(x_ref, bown.at[row], loc_sem.at[1]),
    ]
    barrier = pltpu.get_barrier_semaphore()
    targets = list(y_dev.values()) + list(x_dev.values()) + [c_dev, o_dev, f_dev]
    targets += [dev(x, y, zh, lax.rem(zl + j, NZL), core) for j in range(1, NZL)]
    for t in targets:
        pl.semaphore_signal(barrier, inc=1, device_id=t, device_id_type=MESH)
    for c in own:
        c.start()
    for part in range(4):
        lanes = pl.ds(part * 256, 256)
        for dst, n in ((base_ref, 16), (rot_ref, 8)):
            shape = (n, 256)
            f = lax.broadcasted_iota(jnp.int32, shape, 0) if n == 16 else jnp.full(shape, 16, jnp.int32)
            lag_of = lax.broadcasted_iota(jnp.int32, shape, 1) + (part * 256 - LAGS // 2)
            angle = jnp.bitwise_and(f * lag_of, 2 * FREQ - 1).astype(jnp.float32) * (math.pi / FREQ)
            size = 2.0 / math.sqrt(16.0 * FREQ) if n == 16 else 1.0
            dst[0, :, lanes] = jnp.cos(angle) * size
            dst[1, :, lanes] = jnp.sin(angle) * (-size if n == 16 else size)
    pl.semaphore_wait(barrier, len(targets))

    ints = [
        pltpu.make_async_copy(int_ref, sint.at[0], loc_sem.at[2]),
        pltpu.make_async_copy(pint, sint.at[1], loc_sem.at[3]),
    ]
    beside = pltpu.make_async_copy(abuf.at[pcol], bpar.at[row], loc_sem.at[4])

    i_copy().start()
    ints[0].start()
    o_copy().start()
    near(1, lambda zi: z_send(zi).start())
    near(2, lambda zi: z_send(zi).start())
    near(3, lambda zi: z_send(zi).start())
    f_copy().start()
    t_start(0, 2, 1)
    x_first(0)
    table(0)
    x_first(1)
    o_copy().wait_recv()
    t_start(1, 2, 1)
    t_pass(0, 2, 3, 4)
    x_first(2)
    t_start(2, 1)
    beside.start()
    table(1)
    x_first(3)
    f_copy().wait_recv()
    t_start(3, 1)
    i_copy().wait_recv()
    ints[1].start()
    x_second(0)
    t_wait(0, 3, 4)
    for q in range(3):
        h_copy(q).start()
    t_pass(1, 2, 3, 4)
    table(2)
    x_second(1)
    t_pass(2, 1, 2)
    table(3)
    x_second(2)
    t_pass(3, 1, 2)
    table(4)
    table(5)
    x_second(3)
    table(6)
    table(7)
    for c in ints:
        c.wait()

    rows = lax.broadcasted_iota(jnp.int32, (2 * 16, SLOTS), 0)
    cols = lax.broadcasted_iota(jnp.int32, (2 * 16, SLOTS), 1)
    onehots = []
    for sel in range(2):
        goal = jnp.full((2 * 16, SLOTS), -1, jnp.int32)
        owners = [sint[sel, 0, j] for j in range(SLOTS)]
        for j in range(SLOTS):
            o = owners[j]
            rank = jnp.int32(0)
            for j2 in range(j):
                rank = rank + (o == owners[j2]).astype(jnp.int32)
            ozl = lax.rem(lax.div(o, 2), NZL)
            place = lax.div(o, 8) * 4 + lax.rem(ozl, 2) * 2 + lax.rem(o, 2)
            here = lax.div(ozl, 2) == lax.div(zl, 2)
            at = jnp.where(here, place * 2 + rank, jnp.int32(-1))
            goal = jnp.where(cols == j, at, goal)
        onehots.append((goal == rows).astype(jnp.float32).astype(jnp.bfloat16))

    me = x * 4 + lax.rem(zl, 2) * 2 + core
    columns = (col, pcol)

    def e_copy(i, sel):
        to = lax.rem(me + i, 16)
        tcol = lax.div(to, 4) * 8 + (lax.div(zl, 2) * 2 + lax.rem(lax.div(to, 2), 2)) * 2 + lax.rem(to, 2)
        return remote(
            sbuf.at[sel, to], out_ref.at[:, columns[sel]], es.at[i - 1, sel], er.at[i - 1, sel], (row, tcol)
        )

    def compute(sel, *between):
        def cross(p, _):
            a = abuf[sint[sel, 0, SLOTS + p]].astype(jnp.float32)
            b = (bown, bpar)[sel][sint[sel, 0, 2 * SLOTS + p]].astype(jnp.float32)
            act = jnp.where(p < sint[sel, 0, 3 * SLOTS], jnp.float32(1.0), jnp.float32(0.0))
            for i in range(3):
                for j in range(3):
                    re = None
                    im = None
                    for s in range(2):
                        ar, ai = a[i * 4 + s * 2], a[i * 4 + s * 2 + 1]
                        br, bi = b[j * 4 + s * 2], b[j * 4 + s * 2 + 1]
                        rt = ar * br + ai * bi
                        it = ai * br - ar * bi
                        re = rt if re is None else re + rt
                        im = it if im is None else im + it
                    at = pl.multiple_of(((i * 3 + j) * SLOTS + p) * PITCH, 8)
                    xs[pl.ds(at, 16), :] = re * act
                    xs[pl.ds(at + 16, 16), :] = im * act
            return 0

        def pack(g, _):
            for kk in range(32):
                v = xs[pl.ds(g * (16 * PITCH) + kk, 16, stride=PITCH), :]
                lhs[pl.ds(pl.multiple_of(g * 16, 16), 16), pl.ds(kk * 128, 128)] = v.astype(jnp.bfloat16)
            return 0

        def mm(n, _):
            lanes = pl.ds(pl.multiple_of(n * 256, 256), 256)
            acc = jnp.dot(lhs[...], tab[:, lanes], preferred_element_type=jnp.float32)
            lag[:, lanes] = acc.astype(jnp.bfloat16)
            return 0

        lax.fori_loop(0, SLOTS, cross, 0)
        if len(between) > 1:
            between[1]()
        lax.fori_loop(0, 9, pack, 0)
        if between:
            between[0]()
        lax.fori_loop(0, 4, mm, 0)
        for k in range(9):
            part = lag[pl.ds(k * SLOTS, SLOTS), :]
            v = jnp.dot(onehots[sel], part, preferred_element_type=jnp.float32).astype(jnp.bfloat16)
            sbuf[sel, :, k] = v.reshape(16, 2, LAGS)
        for i in range(1, 16):
            e_copy(i, sel).start()
        mine[sel].start()

    mine = [
        pltpu.make_async_copy(sbuf.at[sel, me], out_ref.at[:, columns[sel]], loc_sem.at[5 + sel])
        for sel in range(2)
    ]
    t_wait(0, 1)
    t_wait(1, 1, 3, 4)
    for q in range(NX * NZL):
        c_copy(q // NZL, q % NZL).wait_recv()
    for c in own:
        c.wait()

    compute(0, lambda: t_pass(3, 2, 3, 4))
    t_wait(2, 2)
    t_wait(3, 3, 4)
    for q in range(3):
        h_copy(q).wait_recv()
    beside.wait()
    compute(1)

    o_copy().wait_send()
    f_copy().wait_send()
    i_copy().wait_send()
    for k in (1, 2, 3):
        near(k, lambda zi: z_send(zi).wait_send())
    for m in range(4):
        for j in kinds(m):
            for d in (1, -1):
                t_copy(m, j, d).wait_send()
    for q in range(3):
        h_copy(q).wait_send()
    for zi in range(NZL):
        for d in (1, -1, 2):
            x_copy(zi, d).wait_send()
    for q in range(NX * NZL):
        c_copy(q // NZL, q % NZL).wait_send()
    for i in range(1, 16):
        for sel in range(2):
            e_copy(i, sel).wait_recv()
    for i in range(1, 16):
        for sel in range(2):
            e_copy(i, sel).wait_send()
    for c in mine:
        c.wait()


def body(spectra, pair_source, pair_partner, pair_owner, pair_count):
    station = spectra.reshape(12, 16, 128)
    ints = jnp.concatenate(
        [pair_owner, pair_source, pair_partner, pair_count, jnp.zeros(127 - 3 * SLOTS, jnp.int32)]
    )
    vmem = pl.BlockSpec(memory_space=pltpu.VMEM)
    dma = pltpu.SemaphoreType.DMA
    out = pl.pallas_call(
        kernel,
        out_shape=jax.ShapeDtypeStruct((9, COLS, 2, LAGS), jnp.bfloat16),
        in_specs=[vmem, vmem],
        out_specs=pl.BlockSpec(memory_space=pl.ANY),
        scratch_shapes=[
            pltpu.VMEM((COLS, 12, 16, 128), jnp.bfloat16),
            pltpu.VMEM((ROWS, 12, 16, 128), jnp.bfloat16),
            pltpu.VMEM((ROWS, 12, 16, 128), jnp.bfloat16),
            pltpu.VMEM((2 * FREQ, LAGS), jnp.bfloat16),
            pltpu.VMEM((2, 16, LAGS), jnp.float32),
            pltpu.VMEM((9 * SLOTS * PITCH, 128), jnp.float32),
            pltpu.VMEM((9 * SLOTS, 2 * FREQ), jnp.bfloat16),
            pltpu.VMEM((9 * SLOTS, LAGS), jnp.bfloat16),
            pltpu.VMEM((2, 16, 9, 2, LAGS), jnp.bfloat16),
            pltpu.VMEM((2, 16, LAGS), jnp.float32),
            pltpu.VMEM((2, 8, LAGS), jnp.float32),
            pltpu.VMEM((1, 128), jnp.int32),
            pltpu.SMEM((2, 1, 128), jnp.int32),
            dma((7,)),
            dma((NZL + 3,)), dma((NZL + 3,)),
            dma((4, 2, 4)), dma((4, 2, 4)),
            dma((3,)), dma((3,)),
            dma((NZL, 3)), dma((NZL, 3)),
            dma((16,)), dma((16,)),
            dma((15, 2)), dma((15, 2)),
        ],
        compiler_params=pltpu.CompilerParams(
            collective_id=0, has_side_effects=True, vmem_limit_bytes=48 * 1024 * 1024
        ),
    )(station, ints.reshape(1, 128))
    return out.reshape(9, COLS * 2, LAGS).transpose(1, 0, 2)


def solution(mesh):
    placed = (
        P(("row", "col"), None, None, None, None),
        P(("row", "col")),
        P(("row", "col")),
        P(("row", "col")),
        P(("row", "col")),
    )
    return jax.shard_map(
        body, mesh=mesh, in_specs=placed, out_specs=P(("row", "col"), None, None), check_vma=False
    )
```

```python
import math

import jax
import jax.numpy as jnp
import numpy as np
from jax import lax
from jax.experimental import pallas as pl
from jax.experimental.pallas import tpu as pltpu
from jax.sharding import PartitionSpec as P

MESH = pl.DeviceIdType.MESH
LAGS = 1024
FREQ = 2048
NX, NZL, NZH, NY = 4, 4, 2, 8
COLS = 32
ROWS = 16
SLOTS = 16
CHUNKS = 8
STEPS = FREQ // 16
PITCH = 40


def kernel(
    x_ref, int_ref,
    out_ref,
    abuf, bown, bpar, tab, state, xs, lhs, lag, sbuf, base_ref, rot_ref, pint, sint,
    loc_sem, zs, zr, ts, tr, hs, hr, xsend, xrecv, ds, dr, es, er,
):
    row = lax.axis_index("row")
    col = lax.axis_index("col")
    zh = lax.div(row, NY)
    y = lax.rem(row, NY)
    x = lax.div(col, 8)
    zl = lax.rem(lax.div(col, 2), NZL)
    core = lax.rem(col, 2)

    def dev(x_, y_, zh_, zl_, c_):
        return (zh_ * NY + y_, x_ * 8 + zl_ * 2 + c_)

    def ymod(v):
        return lax.rem(v + 2 * NY, NY)

    def xmod(v):
        return lax.rem(v + 2 * NX, NX)

    y_dev = {d: dev(x, ymod(y + d), zh, zl, core) for d in (1, -1, 2, -2)}
    x_dev = {d: dev(xmod(x + d), y, zh, zl, core) for d in (1, -1, 2)}
    c_dev = dev(x, y, zh, zl, 1 - core)
    zp = lax.rem(zl + 2, NZL)
    p_dev = dev(x, y, zh, zp, core)
    pcol = x * 8 + zp * 2 + core
    o_dev = dev(x, y, 1 - zh, zl, core)
    f_dev = dev(x, y, 1 - zh, zp, core)

    def half(h):
        return pl.ds(6 * h, 6)

    def remote(src, dst, s, r, target):
        return pltpu.make_async_remote_copy(
            src_ref=src, dst_ref=dst, send_sem=s, recv_sem=r, device_id=target, device_id_type=MESH
        )

    DI = {1: 0, -1: 1}
    XI = {1: 0, -1: 1, 2: 2}

    def kinds(m):
        return (1, 2) if m == 2 else (1, 2, 3, 4)

    def near(k, body):
        if k == 0:
            body(zl)
        else:
            pl.when(zl >= k)(lambda: body(zl - k))
            pl.when(zl + k < NZL)(lambda: body(zl + k))

    def z_send(zi):
        return remote(x_ref, abuf.at[col], zs.at[zi], zr.at[zl], dev(x, y, zh, zi, core))

    def z_recv(zi):
        return remote(x_ref, abuf.at[x * 8 + zi * 2 + core], zs.at[zi], zr.at[zi], dev(x, y, zh, zi, core))

    def o_copy():
        return remote(x_ref, bown.at[row], zs.at[NZL], zr.at[NZL], o_dev)

    def f_copy():
        return remote(x_ref, bpar.at[row], zs.at[NZL + 1], zr.at[NZL + 1], f_dev)

    def i_copy():
        return remote(int_ref, pint, zs.at[NZL + 2], zr.at[NZL + 2], p_dev)

    def t_copy(m, j, d):
        buf = bown if m < 2 else bpar
        back = (0, 0 if m < 2 else 1, 2, 2)[j - 1]
        idx = (zh if m % 2 == 0 else 1 - zh) * NY + ymod(y - back * d)
        dst = buf.at[idx, half(0 if d == 1 else 1)] if j == 4 else buf.at[idx]
        src = dst
        if back == 0 and m == 0:
            src = x_ref
        elif back == 0 and m == 2:
            src = abuf.at[pcol]
        far = 2 if j == 4 or (j == 2 and m < 2) else 1
        return remote(src, dst, ts.at[m, DI[d], j - 1], tr.at[m, DI[d], j - 1], y_dev[far * d])

    def t_start(m, *js):
        for j in js:
            for d in (1, -1):
                t_copy(m, j, d).start()

    def t_wait(m, *js):
        for j in js:
            for d in (1, -1):
                t_copy(m, j, d).wait_recv()

    def t_pass(m, j, *js):
        for d in (1, -1):
            t_copy(m, j, d).wait_recv()
            for j2 in js:
                t_copy(m, j2, d).start()

    def h_copy(q):
        idx = zh * NY + ymod(y + (3, -3, 4)[q])
        return remote(bown.at[idx], bpar.at[idx], hs.at[q], hr.at[q], p_dev)

    def x_copy(zi, d, own=False):
        idx = x * 8 + zi * 2 + core
        src = x_ref if own else abuf.at[idx]
        return remote(src, abuf.at[idx], xsend.at[zi, XI[d]], xrecv.at[zi, XI[d]], x_dev[d])

    def c_copy(xst, zi, own=False):
        idx = xst * 8 + zi * 2 + core
        src = x_ref if own else abuf.at[idx]
        q = xst * NZL + zi
        return remote(src, abuf.at[idx], ds.at[q], dr.at[q], c_dev)

    def x_first(k):
        def body(zi):
            if k:
                z_recv(zi).wait_recv()
            for d in (2, 1, -1):
                x_copy(zi, d, own=k == 0).start()
            c_copy(x, zi, own=k == 0).start()
        near(k, body)

    def x_second(k):
        def body(zi):
            for d in (1, -1, 2):
                x_copy(zi, d).wait_recv()
                c_copy(xmod(x - d), zi).start()
        near(k, body)

    def table(chunk):
        per = STEPS // CHUNKS
        for part in range(4):
            lanes = pl.ds(part * 256, 256)
            rc = jnp.concatenate([rot_ref[0, :, lanes]] * 2, axis=0)
            rs = jnp.concatenate([rot_ref[1, :, lanes]] * 2, axis=0)

            def step(i, cs):
                c, s = cs
                f0 = pl.multiple_of((chunk * per + i) * 16, 16)
                tab[pl.ds(f0, 16), lanes] = c.astype(jnp.bfloat16)
                tab[pl.ds(FREQ + f0, 16), lanes] = s.astype(jnp.bfloat16)
                return (c * rc + s * rs, s * rc - c * rs)

            if chunk == 0:
                init = (base_ref[0, :, lanes], base_ref[1, :, lanes])
            else:
                init = (state[0, :, lanes], state[1, :, lanes])
            c, s = lax.fori_loop(0, per, step, init)
            state[0, :, lanes] = c
            state[1, :, lanes] = s
        if chunk == 0:
            rows = lax.broadcasted_iota(jnp.int32, (16, LAGS), 0)
            weight = jnp.where(rows == 0, 0.5, 1.0)
            tab[pl.ds(0, 16), :] = (base_ref[0] * weight).astype(jnp.bfloat16)
            tab[pl.ds(FREQ, 16), :] = (base_ref[1] * weight).astype(jnp.bfloat16)

    own = [
        pltpu.make_async_copy(x_ref, abuf.at[col], loc_sem.at[0]),
        pltpu.make_async_copy(x_ref, bown.at[row], loc_sem.at[1]),
    ]
    barrier = pltpu.get_barrier_semaphore()
    targets = list(y_dev.values()) + list(x_dev.values()) + [c_dev, o_dev, f_dev]
    targets += [dev(x, y, zh, lax.rem(zl + j, NZL), core) for j in range(1, NZL)]
    for t in targets:
        pl.semaphore_signal(barrier, inc=1, device_id=t, device_id_type=MESH)
    for c in own:
        c.start()
    pl.semaphore_wait(barrier, len(targets))

    ints = [
        pltpu.make_async_copy(int_ref, sint.at[0], loc_sem.at[2]),
        pltpu.make_async_copy(pint, sint.at[1], loc_sem.at[3]),
    ]
    beside = pltpu.make_async_copy(abuf.at[pcol], bpar.at[row], loc_sem.at[4])

    i_copy().start()
    ints[0].start()
    o_copy().start()
    near(1, lambda zi: z_send(zi).start())
    near(2, lambda zi: z_send(zi).start())
    near(3, lambda zi: z_send(zi).start())
    f_copy().start()
    t_start(0, 2, 1)
    x_first(0)
    for part in range(4):
        lanes = pl.ds(part * 256, 256)
        for dst, n in ((base_ref, 16), (rot_ref, 8)):
            shape = (n, 256)
            f = lax.broadcasted_iota(jnp.int32, shape, 0) if n == 16 else jnp.full(shape, 16, jnp.int32)
            lag_of = lax.broadcasted_iota(jnp.int32, shape, 1) + (part * 256 - LAGS // 2)
            angle = jnp.bitwise_and(f * lag_of, 2 * FREQ - 1).astype(jnp.float32) * (math.pi / FREQ)
            size = 2.0 / math.sqrt(16.0 * FREQ) if n == 16 else 1.0
            dst[0, :, lanes] = jnp.cos(angle) * size
            dst[1, :, lanes] = jnp.sin(angle) * (-size if n == 16 else size)
    table(0)
    x_first(1)
    o_copy().wait_recv()
    t_start(1, 2, 1)
    t_pass(0, 2, 3, 4)
    x_first(2)
    t_start(2, 1)
    beside.start()
    table(1)
    x_first(3)
    f_copy().wait_recv()
    t_start(3, 1)
    i_copy().wait_recv()
    ints[1].start()
    x_second(0)
    t_wait(0, 3, 4)
    for q in range(3):
        h_copy(q).start()
    t_pass(1, 2, 3, 4)
    table(2)
    x_second(1)
    t_pass(2, 1, 2)
    table(3)
    x_second(2)
    t_pass(3, 1, 2)
    table(4)
    table(5)
    x_second(3)
    table(6)
    table(7)
    for c in ints:
        c.wait()

    rows = lax.broadcasted_iota(jnp.int32, (2 * 16, SLOTS), 0)
    cols = lax.broadcasted_iota(jnp.int32, (2 * 16, SLOTS), 1)
    onehots = []
    for sel in range(2):
        goal = jnp.full((2 * 16, SLOTS), -1, jnp.int32)
        owners = [sint[sel, 0, j] for j in range(SLOTS)]
        for j in range(SLOTS):
            o = owners[j]
            rank = jnp.int32(0)
            for j2 in range(j):
                rank = rank + (o == owners[j2]).astype(jnp.int32)
            ozl = lax.rem(lax.div(o, 2), NZL)
            place = lax.div(o, 8) * 4 + lax.rem(ozl, 2) * 2 + lax.rem(o, 2)
            here = lax.div(ozl, 2) == lax.div(zl, 2)
            at = jnp.where(here, place * 2 + rank, jnp.int32(-1))
            goal = jnp.where(cols == j, at, goal)
        onehots.append((goal == rows).astype(jnp.float32).astype(jnp.bfloat16))

    me = x * 4 + lax.rem(zl, 2) * 2 + core
    columns = (col, pcol)

    def e_copy(i, sel):
        to = lax.rem(me + i, 16)
        tcol = lax.div(to, 4) * 8 + (lax.div(zl, 2) * 2 + lax.rem(lax.div(to, 2), 2)) * 2 + lax.rem(to, 2)
        return remote(
            sbuf.at[sel, to], out_ref.at[:, columns[sel]], es.at[i - 1, sel], er.at[i - 1, sel], (row, tcol)
        )

    def compute(sel, *between):
        def cross(p, _):
            a = abuf[sint[sel, 0, SLOTS + p]].astype(jnp.float32)
            b = (bown, bpar)[sel][sint[sel, 0, 2 * SLOTS + p]].astype(jnp.float32)
            act = jnp.where(p < sint[sel, 0, 3 * SLOTS], jnp.float32(1.0), jnp.float32(0.0))
            for i in range(3):
                for j in range(3):
                    re = None
                    im = None
                    for s in range(2):
                        ar, ai = a[i * 4 + s * 2], a[i * 4 + s * 2 + 1]
                        br, bi = b[j * 4 + s * 2], b[j * 4 + s * 2 + 1]
                        rt = ar * br + ai * bi
                        it = ai * br - ar * bi
                        re = rt if re is None else re + rt
                        im = it if im is None else im + it
                    at = pl.multiple_of(((i * 3 + j) * SLOTS + p) * PITCH, 8)
                    xs[pl.ds(at, 16), :] = re * act
                    xs[pl.ds(at + 16, 16), :] = im * act
            return 0

        def pack(g, _):
            for kk in range(32):
                v = xs[pl.ds(g * (16 * PITCH) + kk, 16, stride=PITCH), :]
                lhs[pl.ds(pl.multiple_of(g * 16, 16), 16), pl.ds(kk * 128, 128)] = v.astype(jnp.bfloat16)
            return 0

        def mm(n, _):
            lanes = pl.ds(pl.multiple_of(n * 256, 256), 256)
            acc = jnp.dot(lhs[...], tab[:, lanes], preferred_element_type=jnp.float32)
            lag[:, lanes] = acc.astype(jnp.bfloat16)
            return 0

        lax.fori_loop(0, SLOTS, cross, 0)
        if len(between) > 1:
            between[1]()
        lax.fori_loop(0, 9, pack, 0)
        if between:
            between[0]()
        lag[...] = jnp.dot(lhs[...], tab[...], preferred_element_type=jnp.float32).astype(jnp.bfloat16)
        for k in range(9):
            part = lag[pl.ds(k * SLOTS, SLOTS), :]
            v = jnp.dot(onehots[sel], part, preferred_element_type=jnp.float32).astype(jnp.bfloat16)
            sbuf[sel, :, k] = v.reshape(16, 2, LAGS)
        for i in range(1, 16):
            e_copy(i, sel).start()
        mine[sel].start()

    mine = [
        pltpu.make_async_copy(sbuf.at[sel, me], out_ref.at[:, columns[sel]], loc_sem.at[5 + sel])
        for sel in range(2)
    ]
    t_wait(0, 1)
    t_wait(1, 1, 3, 4)
    for q in range(NX * NZL):
        c_copy(q // NZL, q % NZL).wait_recv()
    for c in own:
        c.wait()

    compute(0, lambda: t_pass(3, 2, 3, 4))
    t_wait(2, 2)
    t_wait(3, 3, 4)
    for q in range(3):
        h_copy(q).wait_recv()
    beside.wait()
    compute(1)

    o_copy().wait_send()
    f_copy().wait_send()
    i_copy().wait_send()
    for k in (1, 2, 3):
        near(k, lambda zi: z_send(zi).wait_send())
    for m in range(4):
        for j in kinds(m):
            for d in (1, -1):
                t_copy(m, j, d).wait_send()
    for q in range(3):
        h_copy(q).wait_send()
    for zi in range(NZL):
        for d in (1, -1, 2):
            x_copy(zi, d).wait_send()
    for q in range(NX * NZL):
        c_copy(q // NZL, q % NZL).wait_send()
    for i in range(1, 16):
        for sel in range(2):
            e_copy(i, sel).wait_recv()
    for i in range(1, 16):
        for sel in range(2):
            e_copy(i, sel).wait_send()
    for c in mine:
        c.wait()


def body(spectra, pair_source, pair_partner, pair_owner, pair_count):
    station = spectra.reshape(12, 16, 128)
    ints = jnp.concatenate(
        [pair_owner, pair_source, pair_partner, pair_count, jnp.zeros(127 - 3 * SLOTS, jnp.int32)]
    )
    vmem = pl.BlockSpec(memory_space=pltpu.VMEM)
    dma = pltpu.SemaphoreType.DMA
    out = pl.pallas_call(
        kernel,
        out_shape=jax.ShapeDtypeStruct((9, COLS, 2, LAGS), jnp.bfloat16),
        in_specs=[vmem, vmem],
        out_specs=pl.BlockSpec(memory_space=pl.ANY),
        scratch_shapes=[
            pltpu.VMEM((COLS, 12, 16, 128), jnp.bfloat16),
            pltpu.VMEM((ROWS, 12, 16, 128), jnp.bfloat16),
            pltpu.VMEM((ROWS, 12, 16, 128), jnp.bfloat16),
            pltpu.VMEM((2 * FREQ, LAGS), jnp.bfloat16),
            pltpu.VMEM((2, 16, LAGS), jnp.float32),
            pltpu.VMEM((9 * SLOTS * PITCH, 128), jnp.float32),
            pltpu.VMEM((9 * SLOTS, 2 * FREQ), jnp.bfloat16),
            pltpu.VMEM((9 * SLOTS, LAGS), jnp.bfloat16),
            pltpu.VMEM((2, 16, 9, 2, LAGS), jnp.bfloat16),
            pltpu.VMEM((2, 16, LAGS), jnp.float32),
            pltpu.VMEM((2, 8, LAGS), jnp.float32),
            pltpu.VMEM((1, 128), jnp.int32),
            pltpu.SMEM((2, 1, 128), jnp.int32),
            dma((7,)),
            dma((NZL + 3,)), dma((NZL + 3,)),
            dma((4, 2, 4)), dma((4, 2, 4)),
            dma((3,)), dma((3,)),
            dma((NZL, 3)), dma((NZL, 3)),
            dma((16,)), dma((16,)),
            dma((15, 2)), dma((15, 2)),
        ],
        compiler_params=pltpu.CompilerParams(
            collective_id=0, has_side_effects=True, vmem_limit_bytes=48 * 1024 * 1024
        ),
    )(station, ints.reshape(1, 128))
    return out.reshape(9, COLS * 2, LAGS).transpose(1, 0, 2)


def solution(mesh):
    placed = (
        P(("row", "col"), None, None, None, None),
        P(("row", "col")),
        P(("row", "col")),
        P(("row", "col")),
        P(("row", "col")),
    )
    return jax.shard_map(
        body, mesh=mesh, in_specs=placed, out_specs=P(("row", "col"), None, None), check_vma=False
    )
```
